32 devices in a mesh: frag: 2 (over y), orb: 16 (over z, x, core).
Axes of the slice: x: 2, y: 2, z: 4, core: 2. Of those that a mesh axis runs over, the one named last changes fastest.
Arguments:
- slices: float32 [32, 640, 1024], P(('frag', 'orb')), parts along dimension 0, may hold values from -0.5 to 0.5
- occ_energy: float32 [32], P('frag'), parts along dimension 0, may hold values from -2 to -0.5
- virt_energy: float32 [1280], P('frag'), parts along dimension 0, may hold values from 0.3 to 3
- order: int32 [32], P('frag'), parts along dimension 0, may hold values from 0 to 15, each once
- near_keep: int32 [32], P(('frag', 'orb')), parts along dimension 0, may hold values 0 or 1
- far_keep: int32 [16], P('frag'), parts along dimension 0, may hold values 0 or 1
Outputs:
- density: float32 [32, 640, 1024], P(('frag', 'orb')), parts along dimension 0
The draws below stay inside these ranges and needn't reach their ends.
There are 2 independent parts, one for each index of `frag`. The reference program is written for one: setup_inputs(seed, part) draws one part's arguments, and reference() takes and returns one part's arrays. A program takes and returns all parts, laid end to end along the dimension named above; each array names one. Nothing has to cross between parts.
Inputs may be any that keep to these rules, and one draw needn't show every extreme that they name: `order`: each position gets a different energy index.
All inputs are finite; a program needn't handle non-finite values. No bound on the sum of `near_keep` on one device may be relied on, other than what follows from the above.
Results may differ from the reference program's by a relative error of at most 0.0003.
Values sent between devices are 32-bit elements; how exact they have to be, the bound alone decides.
No kernel may reach another device: no remote copies, remote signals or barrier semaphores. Data moves between devices by JAX's collectives and lax.ppermute only.
A program may use at most 128 MiB of HBM per device.

```python
import jax
import jax.numpy as jnp
from jax import lax

NV = 640
NAUX = 1024
NOCC = 16


def set_ends(result, rng, smallest, top_value):
    index_at = [jax.random.randint(jax.random.fold_in(rng, axis), (), 0, length) for axis, length in enumerate(result.shape)]
    main_axis = result.shape.index(max(result.shape))
    neighbour = index_at[:main_axis] + [(index_at[main_axis] + 1) % result.shape[main_axis]] + index_at[main_axis + 1:]
    return result.at[tuple(index_at)].set(smallest).at[tuple(neighbour)].set(top_value)


def shard_levels(own_key, dims, cuts, low, largest):
    def one(axis_at, blocks):
        draws = jax.random.uniform(jax.random.fold_in(jax.random.fold_in(own_key, 6), axis_at), (blocks,), jnp.float32, low / len(cuts), largest / len(cuts))
        return jnp.repeat(jnp.exp(draws), dims[axis_at] // blocks).reshape((-1,) + (1,) * (len(dims) - axis_at - 1))

    level = one(*cuts[0])
    for cut in cuts[1:]:
        level = level * one(*cut)
    return level


def normal_values(stream_key, extent, scale, most, shards=(), held_as=jnp.bfloat16):
    result = jax.random.normal(stream_key, extent, jnp.float32) * scale
    if len(shards) > 0:
        result = shard_levels(stream_key, extent, shards, -0.22, 0.18) * result
    return jnp.clip(result, min=-most, max=most).astype(held_as)


def setup_inputs(seed: int = 0, part: int = 0) -> dict:
    key_list = jax.random.split(jax.random.key(seed), 7)
    part_splits = jax.random.split(jax.random.fold_in(key_list[6], part), 7)
    slices = normal_values(part_splits[0], (NOCC, NV, NAUX), 0.08, 0.5, ((0, 16),), jnp.float32)
    occ_energy = jnp.clip(jax.random.uniform(part_splits[1], (NOCC,), jnp.float32, -2.0, -0.5), -2.0, -0.5)
    virt_energy = jnp.clip(jax.random.uniform(part_splits[2], (NV,), jnp.float32, 0.3, 3.0), 0.3, 3.0)
    order = jax.random.permutation(part_splits[3], NOCC).astype(jnp.int32)
    near_keep = set_ends((jax.random.randint(part_splits[4], (NOCC,), 0, 4) < 3).astype(jnp.int32), jax.random.fold_in(part_splits[4], 1), 0, 1)
    far_keep = set_ends((jax.random.randint(part_splits[5], (NOCC // 2,), 0, 4) < 3).astype(jnp.int32), jax.random.fold_in(part_splits[5], 1), 0, 1)
    return {"slices": slices, "occ_energy": occ_energy, "virt_energy": virt_energy, "order": order, "near_keep": near_keep, "far_keep": far_keep}


def amplitudes(left, right, left_energy, right_energy, virtual):
    coupling = lax.dot_general(left, right, (((1,), (1,)), ((), ())), precision=lax.Precision.HIGHEST, preferred_element_type=jnp.float32)
    denom = left_energy + right_energy - virtual[:, None] - virtual[None, :]
    scaled = coupling / denom
    return 2.0 * scaled - scaled.T


def matmul(left, right):
    return jnp.dot(left, right, precision=lax.Precision.HIGHEST, preferred_element_type=jnp.float32)


def reference(slices, occ_energy, virt_energy, order, near_keep, far_keep):
    energy = jnp.take(occ_energy, order)
    middle = NOCC // 2

    def one_orbital(orbital):
        orbital = orbital.astype(jnp.int32)
        next_index = ((orbital + 1) % NOCC).astype(jnp.int32)
        far_index = ((orbital + middle) % NOCC).astype(jnp.int32)
        own = lax.dynamic_index_in_dim(slices, orbital, 0, keepdims=False)
        nearby = lax.dynamic_index_in_dim(slices, next_index, 0, keepdims=False)
        facing = lax.dynamic_index_in_dim(slices, far_index, 0, keepdims=False)
        own_energy = lax.dynamic_index_in_dim(energy, orbital, 0, keepdims=False)
        next_energy = lax.dynamic_index_in_dim(energy, next_index, 0, keepdims=False)
        far_energy = lax.dynamic_index_in_dim(energy, far_index, 0, keepdims=False)
        near_weight = lax.dynamic_index_in_dim(near_keep, orbital, 0, keepdims=False).astype(jnp.float32)
        far_weight = lax.dynamic_index_in_dim(far_keep, (orbital % middle).astype(jnp.int32), 0, keepdims=False).astype(jnp.float32)
        diag_amps = amplitudes(own, own, own_energy, own_energy, virt_energy)
        near_amps = amplitudes(own, nearby, own_energy, next_energy, virt_energy) * near_weight
        far_amps = amplitudes(own, facing, own_energy, far_energy, virt_energy) * far_weight
        mine = matmul(diag_amps, own) + matmul(near_amps, nearby) + matmul(far_amps, facing)
        partner = lax.dot_general(near_amps, own, (((0,), (0,)), ((), ())), precision=lax.Precision.HIGHEST, preferred_element_type=jnp.float32)
        return mine, partner

    mine, partner = lax.map(one_orbital, jnp.arange(NOCC, dtype=jnp.int32))
    return mine + jnp.roll(partner, 1, axis=0)
```

```python
import jax
import jax.numpy as jnp
from jax import lax
from jax.experimental import pallas as pl
from jax.experimental.pallas import tpu as pltpu
from jax.sharding import PartitionSpec as P


NT = (((1,), (1,)), ((), ()))
NN = (((1,), (0,)), ((), ()))


def permute(block, pairs):
    return lax.ppermute(block, "orb", pairs)


def both_ways(pairs):
    return pairs + [(j, i) for i, j in pairs]


def split(x):
    high = x.astype(jnp.bfloat16)
    low = (x - high.astype(jnp.float32)).astype(jnp.bfloat16)
    return high, low


def put_left(ref, rows, x):
    high, low = split(x)
    k = x.shape[1]
    ref[rows, 0:k] = high
    ref[rows, k : 2 * k] = high
    ref[rows, 2 * k : 3 * k] = low


def put_right(ref, rows, x):
    high, low = split(x)
    k = x.shape[1]
    ref[rows, 0:k] = high
    ref[rows, k : 2 * k] = low
    ref[rows, 2 * k : 3 * k] = high


def dot(left, right, dims):
    return lax.dot_general(left, right, dims, preferred_element_type=jnp.float32)


def scalars(slot, order, occ, near, prev_near, far):
    n = lax.axis_size("orb")
    m = n // 2
    pos = lax.axis_index("orb")
    odd = lax.rem(pos, 2) == 1
    half = lax.rem(pos, m)
    special = (half == 0) | (half == m - 1)
    mate = jnp.where(odd, pos - 1, pos + 1)
    outer = lax.rem(jnp.where(odd, pos + 1, pos + n - 1), n)
    opposite = lax.rem(pos + m, n)
    if slot == "D":
        partner, weight = pos, jnp.float32(1.0)
    else:
        near_next = near[0].astype(jnp.float32)
        near_before = prev_near[0]
        mate_weight = jnp.where(odd, near_before, near_next)
        outer_weight = jnp.where(odd, near_next, near_before)
        far_weight = far[half].astype(jnp.float32)
        if slot == "A":
            partner, weight = mate, mate_weight
        else:
            ring = jnp.logical_not(special) if slot == "B" else special
            partner = jnp.where(ring, outer, opposite)
            weight = jnp.where(ring, outer_weight, far_weight)
    return occ[order[pos]] + occ[order[partner]], weight, special


def pair_kernel(slot, order, occ, near, prev_near, far, own, *rest):
    rest = list(rest)
    others = [own] if slot == "D" else [rest.pop(0) for _ in range(1 if slot == "A" else 2 if slot == "B" else 4)]
    vrow, vcol = rest.pop(0), rest.pop(0)
    acc = None if slot == "D" else rest.pop(0)
    out, left, right, wide, tall = rest
    total, weight, special = scalars(slot, order, occ, near, prev_near, far)
    put_left(left, slice(None), own[...])
    if slot in "DA":
        parts = [others[0][...]]
    elif slot == "B":
        parts = [jnp.where(special, others[1][...], others[0][...])]
    else:
        parts = [jnp.where(special, others[1][...], others[0][...]), jnp.where(special, others[3][...], others[2][...])]
    row = 0
    rows = own.shape[0]
    for part in parts:
        put_right(right, slice(row, row + part.shape[0]), part)
        row += part.shape[0]
    k = own.shape[1]
    coupling = dot(left[...], right[...], NT)
    amp = coupling / (total - vcol[...] - vrow[...])
    if slot == "D":
        tilde = amp
    else:
        tilde = (2.0 * amp - amp.T) * weight
    put_left(wide, slice(None), tilde)
    for i in range(3):
        tall[i * rows : (i + 1) * rows, :] = right[:, i * k : (i + 1) * k]
    result = dot(wide[...], tall[...], NN)
    if slot == "D":
        out[...] = result
    else:
        out[...] = acc[...] + result


def pair(slot, small, own, others, vrow, vcol, acc):
    rows, k = own.shape
    smem = pl.BlockSpec(memory_space=pltpu.SMEM)
    vmem = pl.BlockSpec(memory_space=pltpu.VMEM)
    operands = [*small, own, *others, vrow, vcol] + ([] if acc is None else [acc])
    in_specs = [smem] * len(small) + [vmem] * (len(operands) - len(small))
    return pl.pallas_call(
        lambda *refs: pair_kernel(slot, *refs),
        out_shape=jax.ShapeDtypeStruct((rows, k), jnp.float32),
        in_specs=in_specs,
        out_specs=vmem,
        scratch_shapes=[
            pltpu.VMEM((rows, 3 * k), jnp.bfloat16),
            pltpu.VMEM((rows, 3 * k), jnp.bfloat16),
            pltpu.VMEM((rows, 3 * rows), jnp.bfloat16),
            pltpu.VMEM((3 * rows, k), jnp.bfloat16),
        ],
        cost_estimate=pl.CostEstimate(
            flops=12 * rows * rows * k, bytes_accessed=12 * rows * k, transcendentals=0
        ),
    )(*operands)


def after(values, token):
    *values, token = lax.optimization_barrier((*values, token))
    return values, token


def body(slices, occ_energy, virt_energy, order, near_keep, far_keep):
    n = lax.axis_size("orb")
    m = n // 2
    specials = (0, m - 1, m, n - 1)
    mates = [(i, i ^ 1) for i in range(n)]
    outers = both_ways([(i, i + 1) for i in range(1, n - 1, 2) if i not in specials])
    straight = both_ways([(0, m), (m - 1, n - 1)])
    opposites = [(i, (i + m) % n) for i in range(n) if i not in specials]
    forwards = both_ways([(0, m - 1), (m, n - 1)])

    own = slices[0]
    rows = own.shape[0]
    cut = rows // 5 * 3
    pieces = (own[:cut], own[cut:])
    vrow = virt_energy[None, :]
    vcol = virt_energy[:, None]

    s0 = permute(pieces[0], straight)
    s1 = permute(pieces[1], straight)
    mate = permute(own, mates)
    prev_near = permute(near_keep.astype(jnp.float32), [(i, (i + 1) % n) for i in range(n)])
    outer = permute(own, outers)
    small = (order, occ_energy, near_keep, prev_near, far_keep)

    acc = pair("D", (order, occ_energy, near_keep, near_keep, far_keep), own, [], vrow, vcol, None)
    (s0w,), acc = after((s0,), acc)
    w0 = permute(s0w, forwards)
    acc = pair("A", small, own, [mate], vrow, vcol, acc)
    pieces, acc = after(pieces, acc)
    r0 = permute(pieces[0], opposites)
    r1 = permute(pieces[1], opposites)
    w1 = permute(s1, forwards)
    acc = pair("B", small, own, [outer, jnp.concatenate([s0, s1], axis=0)], vrow, vcol, acc)
    acc = pair("L", small, own, [r0, w0, r1, w1], vrow, vcol, acc)
    return acc[None]


def solution(mesh):
    return jax.shard_map(
        body,
        mesh=mesh,
        in_specs=(
            P(("frag", "orb"), None, None),
            P("frag"),
            P("frag"),
            P("frag"),
            P(("frag", "orb")),
            P("frag"),
        ),
        out_specs=P(("frag", "orb"), None, None),
        check_vma=False,
    )
```

```python
import jax
import jax.numpy as jnp
from jax import lax
from jax.experimental import pallas as pl
from jax.experimental.pallas import tpu as pltpu
from jax.sharding import PartitionSpec as P


NT = (((1,), (1,)), ((), ()))
NN = (((1,), (0,)), ((), ()))


def permute(block, pairs):
    return lax.ppermute(block, "orb", pairs)


def both_ways(pairs):
    return pairs + [(j, i) for i, j in pairs]


def split(x):
    high = x.astype(jnp.bfloat16)
    low = (x - high.astype(jnp.float32)).astype(jnp.bfloat16)
    return high, low


def dot(left, right, dims):
    return lax.dot_general(left, right, dims, preferred_element_type=jnp.float32)


def put_wide(ref, x):
    high, low = split(x)
    k = x.shape[1]
    ref[:, 0:k] = high
    ref[:, k : 2 * k] = low
    ref[:, 2 * k : 3 * k] = high


def put_tall(ref, x):
    high, low = split(x)
    k = x.shape[0]
    ref[0:k] = high
    ref[k : 2 * k] = high
    ref[2 * k : 3 * k] = low


def product(wide, tall):
    return dot(wide[...], tall[...], NN)


def overlap(pair, tall):
    k = tall.shape[1]
    rows = tall.shape[0] // 3
    both = dot(pair[...], jnp.concatenate([tall[0:rows], tall[rows : 2 * rows]], axis=1), NT)
    return both + dot(pair[:, 0:k], tall[2 * rows : 3 * rows], NT)


def scalars(slot, order, occ, near, prev_near, far):
    n = lax.axis_size("orb")
    m = n // 2
    pos = lax.axis_index("orb")
    odd = lax.rem(pos, 2) == 1
    half = lax.rem(pos, m)
    special = (half == 0) | (half == m - 1)
    mate = jnp.where(odd, pos - 1, pos + 1)
    outer = lax.rem(jnp.where(odd, pos + 1, pos + n - 1), n)
    opposite = lax.rem(pos + m, n)
    if slot == "D":
        partner, weight = pos, jnp.float32(1.0)
    else:
        near_next = near[0].astype(jnp.float32)
        near_before = prev_near[0]
        mate_weight = jnp.where(odd, near_before, near_next)
        outer_weight = jnp.where(odd, near_next, near_before)
        far_weight = far[half].astype(jnp.float32)
        if slot == "A":
            partner, weight = mate, mate_weight
        else:
            ring = jnp.logical_not(special) if slot == "B" else special
            partner = jnp.where(ring, outer, opposite)
            weight = jnp.where(ring, outer_weight, far_weight)
    return occ[order[pos]] + occ[order[partner]], weight


def case(name):
    n = lax.axis_size("orb")
    m = n // 2
    half = lax.rem(lax.axis_index("orb"), m)
    special = (half == 0) | (half == m - 1)
    return special if name == "special" else jnp.logical_not(special)


def fetch(buffer, sem, sources):
    for name, source in sources:

        @pl.when(case(name))
        def _(source=source):
            copy = pltpu.make_async_copy(source, buffer, sem)
            copy.start()
            copy.wait()


def kernel_d(order, occ, own, vrow, vcol, out, own_pair, wide, tall):
    k = own.shape[1]
    high, low = split(own[...])
    own_pair[:, 0:k] = high
    own_pair[:, k : 2 * k] = low
    put_tall(tall, own[...])
    total, _ = scalars("D", order, occ, None, None, None)
    amp = overlap(own_pair, tall) / (total - vcol[...] - vrow[...])
    put_wide(wide, amp)
    out[...] = product(wide, tall)


def kernel_ab(slot, order, occ, near, prev_near, far, own_pair, *rest):
    *sources, vrow, vcol, acc, out, other, wide, tall, sem = rest
    if slot == "A":
        copy = pltpu.make_async_copy(sources[0], other, sem)
        copy.start()
        copy.wait()
    else:
        cut = sources[1].shape[0]
        fetch(other, sem, [("plain", sources[0])])
        fetch(other.at[0:cut], sem, [("special", sources[1])])
        fetch(other.at[cut:], sem, [("special", sources[2])])
    put_tall(tall, other[...])
    total, weight = scalars(slot, order, occ, near, prev_near, far)
    amp = overlap(own_pair, tall) / (total - vcol[...] - vrow[...])
    put_wide(wide, (2.0 * amp - amp.T) * weight)
    out[...] = acc[...] + product(wide, tall)


def kernel_l0(order, occ, near, prev_near, far, own_pair, late, rest, vrow, vcol, acc, out, amp_a, tall, other, wide, sem):
    cut = rest.shape[0]
    fetch(
        other,
        sem,
        [("special", late), ("plain", rest)],
    )
    put_tall(tall, other[...])
    total, weight = scalars("L", order, occ, near, prev_near, far)
    amp = overlap(own_pair, tall) / (total - vcol[...] - vrow[:, 0:cut])
    amp_a[...] = amp
    inner = amp[0:cut]
    put_wide(wide, (2.0 * inner - inner.T) * weight)
    out[0:cut] = acc[0:cut] + product(wide, tall)
    out[cut:] = acc[cut:]


def kernel_l1(
    order, occ, near, prev_near, far, own_pair, late, rest, vrow, vcol, acc, amp_a, tall_a,
    out, other, tall, wide_ab, wide_ba, wide_bb, sem,
):
    cut = amp_a.shape[1]
    fetch(
        other,
        sem,
        [("special", late), ("plain", rest)],
    )
    put_tall(tall, other[...])
    total, weight = scalars("L", order, occ, near, prev_near, far)
    amp = overlap(own_pair, tall) / (total - vcol[...] - vrow[:, cut:])
    across = amp_a[cut:]
    put_wide(wide_ab, (2.0 * amp[0:cut] - across.T) * weight)
    put_wide(wide_ba, (2.0 * across - amp[0:cut].T) * weight)
    put_wide(wide_bb, (2.0 * amp[cut:] - amp[cut:].T) * weight)
    out[0:cut] = acc[0:cut] + product(wide_ab, tall)
    out[cut:] = acc[cut:] + product(wide_ba, tall_a) + product(wide_bb, tall)


SMEM = pl.BlockSpec(memory_space=pltpu.SMEM)
VMEM = pl.BlockSpec(memory_space=pltpu.VMEM)
ANY = pl.BlockSpec(memory_space=pl.ANY)


def call(kernel, operands, outs, scratch, flops, limit=None):
    return pl.pallas_call(
        kernel,
        out_shape=[jax.ShapeDtypeStruct(shape, dtype) for shape, dtype in outs],
        in_specs=[spec for spec, _ in operands],
        out_specs=[VMEM] * len(outs),
        scratch_shapes=scratch,
        cost_estimate=pl.CostEstimate(flops=flops, bytes_accessed=8_000_000, transcendentals=0),
        compiler_params=pltpu.CompilerParams(vmem_limit_bytes=limit),
    )(*[value for _, value in operands])


def after(values, token):
    *values, token = lax.optimization_barrier((*values, token))
    return values, token


def body(slices, occ_energy, virt_energy, order, near_keep, far_keep):
    n = lax.axis_size("orb")
    m = n // 2
    specials = (0, m - 1, m, n - 1)
    mates = [(i, i ^ 1) for i in range(n)]
    outers = both_ways([(i, i + 1) for i in range(1, n - 1, 2) if i not in specials])
    straight = both_ways([(0, m), (m - 1, n - 1)])
    opposites = [(i, (i + m) % n) for i in range(n) if i not in specials]
    forwards = both_ways([(0, m - 1), (m, n - 1)])

    own = slices[0]
    rows, k = own.shape
    cut = rows // 5 * 3
    size = rows - cut
    bf16, f32 = jnp.bfloat16, jnp.float32
    pieces = (own[:cut], own[cut:])
    v = [(VMEM, virt_energy[None, :]), (VMEM, virt_energy[:, None])]
    flops = 12 * rows * rows * k

    prev_near = permute(near_keep.astype(f32), [(i, (i + 1) % n) for i in range(n)])
    straight_slices = [permute(pieces[0], straight), permute(pieces[1], straight)]
    mate = permute(own, mates)
    outer = permute(own, outers)
    small = [(SMEM, x) for x in (order, occ_energy, near_keep, prev_near, far_keep)]

    acc, own_pair = call(
        kernel_d, [small[0], small[1], (VMEM, own), *v],
        [((rows, k), f32), ((rows, 2 * k), bf16)],
        [pltpu.VMEM((rows, 3 * rows), bf16), pltpu.VMEM((3 * rows, k), bf16)],
        flops,
    )
    whole_scratch = [
        pltpu.VMEM((rows, k), f32),
        pltpu.VMEM((rows, 3 * rows), bf16),
        pltpu.VMEM((3 * rows, k), bf16),
        pltpu.SemaphoreType.DMA,
    ]
    (first, *pieces), acc = after((straight_slices[1], *pieces), acc)
    late1 = permute(first, forwards)
    rest = [permute(piece, opposites) for piece in pieces]
    late = [permute(straight_slices[0], forwards), late1]
    (acc,) = call(
        lambda *refs: kernel_ab("A", *refs),
        [*small, (VMEM, own_pair), (ANY, mate), *v, (VMEM, acc)],
        [((rows, k), f32)], whole_scratch, flops,
    )
    (acc,) = call(
        lambda *refs: kernel_ab("B", *refs),
        [*small, (VMEM, own_pair), (ANY, outer), (ANY, straight_slices[0]), (ANY, straight_slices[1]), *v, (VMEM, acc)],
        [((rows, k), f32)], whole_scratch, flops,
    )
    acc, amp_a, tall_a = call(
        kernel_l0,
        [*small, (VMEM, own_pair), (ANY, late[0]), (ANY, rest[0]), *v, (VMEM, acc)],
        [((rows, k), f32), ((rows, cut), f32), ((3 * cut, k), bf16)],
        [pltpu.VMEM((cut, k), f32), pltpu.VMEM((cut, 3 * cut), bf16), pltpu.SemaphoreType.DMA],
        flops // 2,
        26_000_000,
    )
    (acc,) = call(
        kernel_l1,
        [*small, (VMEM, own_pair), (ANY, late[1]), (ANY, rest[1]), *v, (VMEM, acc), (VMEM, amp_a), (VMEM, tall_a)],
        [((rows, k), f32)],
        [
            pltpu.VMEM((size, k), f32),
            pltpu.VMEM((3 * size, k), bf16),
            pltpu.VMEM((cut, 3 * size), bf16),
            pltpu.VMEM((size, 3 * cut), bf16),
            pltpu.VMEM((size, 3 * size), bf16),
            pltpu.SemaphoreType.DMA,
        ],
        flops // 2,
        26_000_000,
    )
    return acc[None]


def solution(mesh):
    return jax.shard_map(
        body,
        mesh=mesh,
        in_specs=(
            P(("frag", "orb"), None, None),
            P("frag"),
            P("frag"),
            P("frag"),
            P(("frag", "orb")),
            P("frag"),
        ),
        out_specs=P(("frag", "orb"), None, None),
        check_vma=False,
    )
```

```python
import jax
import jax.numpy as jnp
from jax import lax
from jax.experimental import pallas as pl
from jax.experimental.pallas import tpu as pltpu
from jax.sharding import PartitionSpec as P


NT = (((1,), (1,)), ((), ()))
NN = (((1,), (0,)), ((), ()))


def permute(block, pairs):
    return lax.ppermute(block, "orb", pairs)


def both_ways(pairs):
    return pairs + [(j, i) for i, j in pairs]


def split(x):
    high = x.astype(jnp.bfloat16)
    low = (x - high.astype(jnp.float32)).astype(jnp.bfloat16)
    return high, low


def dot(left, right, dims):
    return lax.dot_general(left, right, dims, preferred_element_type=jnp.float32)


def put_tall(ref, x):
    high, low = split(x)
    k = x.shape[0]
    ref[0:k] = high
    ref[k : 2 * k] = high
    ref[2 * k : 3 * k] = low


def put_wide(ref, x):
    high, low = split(x)
    k = x.shape[1]
    ref[:, 0:k] = high
    ref[:, k : 2 * k] = low
    ref[:, 2 * k : 3 * k] = high


def overlap(own, right):
    half = own.shape[0] // 2
    return jnp.concatenate(
        [dot(own[0:half], right[...], NT), dot(own[half:], right[...], NT)], axis=0
    )


def column_blocks(k):
    width = k // 4
    return [slice(i * width, (i + 1) * width) for i in range(4)]


def scalars(slot, order, occ, near, prev_near, far):
    n = lax.axis_size("orb")
    m = n // 2
    pos = lax.axis_index("orb")
    odd = lax.rem(pos, 2) == 1
    half = lax.rem(pos, m)
    special = (half == 0) | (half == m - 1)
    mate = jnp.where(odd, pos - 1, pos + 1)
    outer = lax.rem(jnp.where(odd, pos + 1, pos + n - 1), n)
    opposite = lax.rem(pos + m, n)
    if slot == "D":
        partner, weight = pos, jnp.float32(1.0)
    else:
        near_next = near[0].astype(jnp.float32)
        near_before = prev_near[0]
        mate_weight = jnp.where(odd, near_before, near_next)
        outer_weight = jnp.where(odd, near_next, near_before)
        far_weight = far[half].astype(jnp.float32)
        if slot == "A":
            partner, weight = mate, mate_weight
        else:
            ring = jnp.logical_not(special) if slot == "B" else special
            partner = jnp.where(ring, outer, opposite)
            weight = jnp.where(ring, outer_weight, far_weight)
    return occ[order[pos]] + occ[order[partner]], weight


def case(name):
    n = lax.axis_size("orb")
    m = n // 2
    half = lax.rem(lax.axis_index("orb"), m)
    special = (half == 0) | (half == m - 1)
    return special if name == "special" else jnp.logical_not(special)


def fetch(buffer, sem, sources):
    for name, source in sources:

        @pl.when(case(name))
        def _(source=source):
            copy = pltpu.make_async_copy(source, buffer, sem)
            copy.start()
            copy.wait()


def kernel_d(order, occ, own, vrow, vcol, out, own_three, right, wide, tall):
    k = own.shape[1]
    high, low = split(own[...])
    own_three[:, 0:k] = high
    own_three[:, k : 2 * k] = high
    own_three[:, 2 * k : 3 * k] = low
    put_wide(right, own[...])
    put_tall(tall, own[...])
    total, _ = scalars("D", order, occ, None, None, None)
    put_wide(wide, overlap(own_three, right) / (total - vcol[...] - vrow[...]))
    for columns in column_blocks(k):
        out[:, columns] = dot(wide[...], tall[:, columns], NN)


def kernel_ab(slot, *refs):
    if slot == "A":
        order, occ, near, prev_near, far, own, other, vrow, vcol, acc, out, later, right, wide, tall = refs
        total, weight = scalars("A", order, occ, near, prev_near, far)
        for i, name in enumerate("BL"):
            for j, value in enumerate(scalars(name, order, occ, near, prev_near, far)):
                later[2 * i + j : 2 * i + j + 1] = jnp.full((1, later.shape[1]), value, jnp.float32)
    else:
        later, own, plain, special0, special1, vrow, vcol, acc, out, other, right, wide, tall, sem = refs
        total, weight = later[0:1, 0:1], later[1:2, 0:1]
        cut = special0.shape[0]
        fetch(other, sem, [("plain", plain)])
        fetch(other.at[0:cut], sem, [("special", special0)])
        fetch(other.at[cut:], sem, [("special", special1)])
    put_wide(right, other[...])
    put_tall(tall, other[...])
    amp = overlap(own, right) / (total - vcol[...] - vrow[...])
    put_wide(wide, (2.0 * amp - amp.T) * weight)
    for columns in column_blocks(acc.shape[1]):
        out[:, columns] = acc[:, columns] + dot(wide[...], tall[:, columns], NN)


def kernel_l0(later, own, late, rest, vrow, vcol, acc, out, amp_a, tall, other, right, wide, sem):
    cut = rest.shape[0]
    fetch(other, sem, [("special", late), ("plain", rest)])
    put_wide(right, other[...])
    put_tall(tall, other[...])
    total, weight = later[2:3, 0:1], later[3:4, 0:1]
    amp = overlap(own, right) / (total - vcol[...] - vrow[:, 0:cut])
    amp_a[...] = amp
    inner = amp[0:cut]
    put_wide(wide, (2.0 * inner - inner.T) * weight)
    for columns in column_blocks(acc.shape[1]):
        out[0:cut, columns] = acc[0:cut, columns] + dot(wide[...], tall[:, columns], NN)
    out[cut:] = acc[cut:]


def kernel_l1(
    later, own, late, rest, vrow, vcol, acc, amp_a, tall_a,
    out, right, tall, wide_ab, wide_ba, wide_bb, result, out_sems,
):
    cut = amp_a.shape[1]
    other = jnp.where(case("special"), late[...], rest[...])
    put_wide(right, other)
    put_tall(tall, other)
    total, weight = later[2:3, 0:1], later[3:4, 0:1]
    amp = overlap(own, right) / (total - vcol[...] - vrow[:, cut:])
    across = amp_a[cut:]
    put_wide(wide_ab, (2.0 * amp[0:cut] - across.T) * weight)
    put_wide(wide_ba, (2.0 * across - amp[0:cut].T) * weight)
    put_wide(wide_bb, (2.0 * amp[cut:] - amp[cut:].T) * weight)
    copies = []
    for i, columns in enumerate(column_blocks(acc.shape[1])):
        result[0:cut, columns] = acc[0:cut, columns] + dot(wide_ab[...], tall[:, columns], NN)
        result[cut:, columns] = (
            acc[cut:, columns]
            + dot(wide_ba[...], tall_a[:, columns], NN)
            + dot(wide_bb[...], tall[:, columns], NN)
        )
        copies.append(pltpu.make_async_copy(result.at[:, columns], out.at[:, columns], out_sems.at[i]))
        copies[-1].start()
    for copy in copies:
        copy.wait()


SMEM = pl.BlockSpec(memory_space=pltpu.SMEM)
VMEM = pl.BlockSpec(memory_space=pltpu.VMEM)
ANY = pl.BlockSpec(memory_space=pl.ANY)


def call(kernel, operands, outs, scratch, flops, limit=None, out_specs=None):
    return pl.pallas_call(
        kernel,
        out_shape=[jax.ShapeDtypeStruct(shape, dtype) for shape, dtype in outs],
        in_specs=[spec for spec, _ in operands],
        out_specs=out_specs or [VMEM] * len(outs),
        scratch_shapes=scratch,
        cost_estimate=pl.CostEstimate(flops=flops, bytes_accessed=8_000_000, transcendentals=0),
        compiler_params=pltpu.CompilerParams(vmem_limit_bytes=limit),
    )(*[value for _, value in operands])


def piece(array, start, size):
    def kernel(source, out, sem):
        copy = pltpu.make_async_copy(source.at[pl.ds(start, size)], out, sem)
        copy.start()
        copy.wait()

    shape = (size, array.shape[1])
    return call(kernel, [(ANY, array)], [(shape, array.dtype)], [pltpu.SemaphoreType.DMA], 0, 4_000_000)[0]


def after(values, token):
    *values, token = lax.optimization_barrier((*values, token))
    return values, token


def body(slices, occ_energy, virt_energy, order, near_keep, far_keep):
    n = lax.axis_size("orb")
    m = n // 2
    specials = (0, m - 1, m, n - 1)
    mates = [(i, i ^ 1) for i in range(n)]
    outers = both_ways([(i, i + 1) for i in range(1, n - 1, 2) if i not in specials])
    straight = both_ways([(0, m), (m - 1, n - 1)])
    opposites = [(i, (i + m) % n) for i in range(n) if i not in specials]
    forwards = both_ways([(0, m - 1), (m, n - 1)])

    own = slices[0]
    rows, k = own.shape
    cut = rows // 5 * 3
    size = rows - cut
    bf16, f32 = jnp.bfloat16, jnp.float32
    pieces = (piece(own, 0, cut), piece(own, cut, size))
    v = [(VMEM, virt_energy[None, :]), (VMEM, virt_energy[:, None])]
    flops = 12 * rows * rows * k

    prev_near = permute(near_keep.astype(f32), [(i, (i + 1) % n) for i in range(n)])
    straight_slices = [permute(pieces[0], straight), permute(pieces[1], straight)]
    mate = permute(own, mates)
    outer = permute(own, outers)
    small = [(SMEM, x) for x in (order, occ_energy, near_keep, prev_near, far_keep)]

    right = pltpu.VMEM((rows, 3 * k), bf16)
    wide = pltpu.VMEM((rows, 3 * rows), bf16)
    tall = pltpu.VMEM((3 * rows, k), bf16)
    dma = pltpu.SemaphoreType.DMA
    acc, own_three = call(
        kernel_d, [small[0], small[1], (VMEM, own), *v],
        [((rows, k), f32), ((rows, 3 * k), bf16)], [right, wide, tall], flops,
    )
    (first, whole), acc = after((straight_slices[1], own), acc)
    late1 = permute(first, forwards)
    pieces = (whole[:cut], whole[cut:])
    rest = [permute(piece, opposites) for piece in pieces]
    late = [permute(straight_slices[0], forwards), late1]
    acc, later = call(
        lambda *refs: kernel_ab("A", *refs),
        [*small, (VMEM, own_three), (VMEM, mate), *v, (VMEM, acc)],
        [((rows, k), f32), ((8, 128), f32)], [right, wide, tall], flops,
    )
    (acc,) = call(
        lambda *refs: kernel_ab("B", *refs),
        [(VMEM, later), (VMEM, own_three), (ANY, outer), *((ANY, x) for x in straight_slices), *v, (VMEM, acc)],
        [((rows, k), f32)], [pltpu.VMEM((rows, k), f32), right, wide, tall, dma], flops,
    )
    acc, amp_a, tall_a = call(
        kernel_l0,
        [(VMEM, later), (VMEM, own_three), (ANY, late[0]), (ANY, rest[0]), *v, (VMEM, acc)],
        [((rows, k), f32), ((rows, cut), f32), ((3 * cut, k), bf16)],
        [pltpu.VMEM((cut, k), f32), pltpu.VMEM((cut, 3 * k), bf16), pltpu.VMEM((cut, 3 * cut), bf16), dma],
        flops // 2,
        26_000_000,
    )
    (acc,) = call(
        kernel_l1,
        [(VMEM, later), (VMEM, own_three), (VMEM, late[1]), (VMEM, rest[1]), *v, (VMEM, acc), (VMEM, amp_a), (VMEM, tall_a)],
        [((rows, k), f32)],
        [
            pltpu.VMEM((size, 3 * k), bf16),
            pltpu.VMEM((3 * size, k), bf16),
            pltpu.VMEM((cut, 3 * size), bf16),
            pltpu.VMEM((size, 3 * cut), bf16),
            pltpu.VMEM((size, 3 * size), bf16),
            pltpu.VMEM((rows, k), f32),
            pltpu.SemaphoreType.DMA((4,)),
        ],
        flops // 2,
        26_000_000,
        [ANY],
    )
    return acc[None]


def solution(mesh):
    return jax.shard_map(
        body,
        mesh=mesh,
        in_specs=(
            P(("frag", "orb"), None, None),
            P("frag"),
            P("frag"),
            P("frag"),
            P(("frag", "orb")),
            P("frag"),
        ),
        out_specs=P(("frag", "orb"), None, None),
        check_vma=False,
    )
```

```python
import jax
import jax.numpy as jnp
from jax import lax
from jax.experimental import pallas as pl
from jax.experimental.pallas import tpu as pltpu
from jax.sharding import PartitionSpec as P


NT = (((1,), (1,)), ((), ()))
NN = (((1,), (0,)), ((), ()))


def permute(block, pairs):
    return lax.ppermute(block, "orb", pairs)


def both_ways(pairs):
    return pairs + [(j, i) for i, j in pairs]


def split(x):
    high = x.astype(jnp.bfloat16)
    low = (x - high.astype(jnp.float32)).astype(jnp.bfloat16)
    return high, low


def dot(left, right, dims):
    return lax.dot_general(left, right, dims, preferred_element_type=jnp.float32)


def put_tall(ref, x):
    high, low = split(x)
    k = x.shape[0]
    ref[0:k] = high
    ref[k : 2 * k] = high
    ref[2 * k : 3 * k] = low


def put_wide(ref, x):
    high, low = split(x)
    k = x.shape[1]
    ref[:, 0:k] = high
    ref[:, k : 2 * k] = low
    ref[:, 2 * k : 3 * k] = high


def overlap(own, right):
    half = own.shape[0] // 2
    return jnp.concatenate(
        [dot(own[0:half], right[...], NT), dot(own[half:], right[...], NT)], axis=0
    )


def column_blocks(k):
    width = k // 4
    return [slice(i * width, (i + 1) * width) for i in range(4)]


def scalars(slot, order, occ, near, prev_near, far):
    n = lax.axis_size("orb")
    m = n // 2
    pos = lax.axis_index("orb")
    odd = lax.rem(pos, 2) == 1
    half = lax.rem(pos, m)
    special = (half == 0) | (half == m - 1)
    mate = jnp.where(odd, pos - 1, pos + 1)
    outer = lax.rem(jnp.where(odd, pos + 1, pos + n - 1), n)
    opposite = lax.rem(pos + m, n)
    if slot == "D":
        partner, weight = pos, jnp.float32(1.0)
    else:
        near_next = near[0].astype(jnp.float32)
        near_before = prev_near[0]
        mate_weight = jnp.where(odd, near_before, near_next)
        outer_weight = jnp.where(odd, near_next, near_before)
        far_weight = far[half].astype(jnp.float32)
        if slot == "A":
            partner, weight = mate, mate_weight
        else:
            ring = jnp.logical_not(special) if slot == "B" else special
            partner = jnp.where(ring, outer, opposite)
            weight = jnp.where(ring, outer_weight, far_weight)
    return occ[order[pos]] + occ[order[partner]], weight


def case(name):
    n = lax.axis_size("orb")
    m = n // 2
    half = lax.rem(lax.axis_index("orb"), m)
    special = (half == 0) | (half == m - 1)
    return special if name == "special" else jnp.logical_not(special)


def fetch(buffer, sem, sources):
    for name, source in sources:

        @pl.when(case(name))
        def _(source=source):
            copy = pltpu.make_async_copy(source, buffer, sem)
            copy.start()
            copy.wait()


def kernel_d(order, occ, own, vrow, vcol, out, own_three, right, wide, tall):
    k = own.shape[1]
    high, low = split(own[...])
    own_three[:, 0:k] = high
    own_three[:, k : 2 * k] = high
    own_three[:, 2 * k : 3 * k] = low
    put_wide(right, own[...])
    put_tall(tall, own[...])
    total, _ = scalars("D", order, occ, None, None, None)
    put_wide(wide, overlap(own_three, right) / (total - vcol[...] - vrow[...]))
    for columns in column_blocks(k):
        out[:, columns] = dot(wide[...], tall[:, columns], NN)


def kernel_ab(slot, *refs):
    if slot == "A":
        order, occ, near, prev_near, far, own, other, vrow, vcol, acc, out, later, right, wide, tall = refs
        total, weight = scalars("A", order, occ, near, prev_near, far)
        for i, name in enumerate("BL"):
            for j, value in enumerate(scalars(name, order, occ, near, prev_near, far)):
                later[2 * i + j : 2 * i + j + 1] = jnp.full((1, later.shape[1]), value, jnp.float32)
    else:
        later, own, plain, special0, special1, vrow, vcol, acc, out, other, right, wide, tall, sem = refs
        total, weight = later[0:1, 0:1], later[1:2, 0:1]
        cut = special0.shape[0]
        fetch(other, sem, [("plain", plain)])
        fetch(other.at[0:cut], sem, [("special", special0)])
        fetch(other.at[cut:], sem, [("special", special1)])
    put_wide(right, other[...])
    put_tall(tall, other[...])
    amp = overlap(own, right) / (total - vcol[...] - vrow[...])
    put_wide(wide, (2.0 * amp - amp.T) * weight)
    for columns in column_blocks(acc.shape[1]):
        out[:, columns] = acc[:, columns] + dot(wide[...], tall[:, columns], NN)


def kernel_l0(later, own, late0, late1, rest, vrow, vcol, acc, out, amp_a, tall, right, wide):
    cut = rest.shape[0]
    late = jnp.concatenate([late0[...], late1[0 : cut - late0.shape[0]]], axis=0)
    other = jnp.where(case("special"), late, rest[...])
    put_wide(right, other)
    put_tall(tall, other)
    total, weight = later[2:3, 0:1], later[3:4, 0:1]
    amp = overlap(own, right) / (total - vcol[...] - vrow[:, 0:cut])
    amp_a[...] = amp
    inner = amp[0:cut]
    put_wide(wide, (2.0 * inner - inner.T) * weight)
    for columns in column_blocks(acc.shape[1]):
        out[0:cut, columns] = acc[0:cut, columns] + dot(wide[...], tall[:, columns], NN)
    out[cut:] = acc[cut:]


def kernel_l1(
    later, own, late, rest, vrow, vcol, acc, amp_a, tall_a,
    out, right, tall, wide_ab, wide_ba, wide_bb, result, out_sems,
):
    cut = amp_a.shape[1]
    size = rest.shape[0]
    other = jnp.where(case("special"), late[late.shape[0] - size :], rest[...])
    put_wide(right, other)
    put_tall(tall, other)
    total, weight = later[2:3, 0:1], later[3:4, 0:1]
    amp = overlap(own, right) / (total - vcol[...] - vrow[:, cut:])
    across = amp_a[cut:]
    put_wide(wide_ab, (2.0 * amp[0:cut] - across.T) * weight)
    put_wide(wide_ba, (2.0 * across - amp[0:cut].T) * weight)
    put_wide(wide_bb, (2.0 * amp[cut:] - amp[cut:].T) * weight)
    copies = []
    for i, columns in enumerate(column_blocks(acc.shape[1])):
        result[0:cut, columns] = acc[0:cut, columns] + dot(wide_ab[...], tall[:, columns], NN)
        result[cut:, columns] = (
            acc[cut:, columns]
            + dot(wide_ba[...], tall_a[:, columns], NN)
            + dot(wide_bb[...], tall[:, columns], NN)
        )
        copies.append(pltpu.make_async_copy(result.at[:, columns], out.at[:, columns], out_sems.at[i]))
        copies[-1].start()
    for copy in copies:
        copy.wait()


SMEM = pl.BlockSpec(memory_space=pltpu.SMEM)
VMEM = pl.BlockSpec(memory_space=pltpu.VMEM)
ANY = pl.BlockSpec(memory_space=pl.ANY)


def call(kernel, operands, outs, scratch, flops, limit=None, out_specs=None):
    return pl.pallas_call(
        kernel,
        out_shape=[jax.ShapeDtypeStruct(shape, dtype) for shape, dtype in outs],
        in_specs=[spec for spec, _ in operands],
        out_specs=out_specs or [VMEM] * len(outs),
        scratch_shapes=scratch,
        cost_estimate=pl.CostEstimate(flops=flops, bytes_accessed=8_000_000, transcendentals=0),
        compiler_params=pltpu.CompilerParams(vmem_limit_bytes=limit),
    )(*[value for _, value in operands])


def piece(array, start, size):
    def kernel(source, out, sem):
        copy = pltpu.make_async_copy(source.at[pl.ds(start, size)], out, sem)
        copy.start()
        copy.wait()

    shape = (size, array.shape[1])
    return call(kernel, [(ANY, array)], [(shape, array.dtype)], [pltpu.SemaphoreType.DMA], 0, 4_000_000)[0]


def after(values, token):
    *values, token = lax.optimization_barrier((*values, token))
    return values, token


def body(slices, occ_energy, virt_energy, order, near_keep, far_keep):
    n = lax.axis_size("orb")
    m = n // 2
    specials = (0, m - 1, m, n - 1)
    mates = [(i, i ^ 1) for i in range(n)]
    outers = both_ways([(i, i + 1) for i in range(1, n - 1, 2) if i not in specials])
    straight = both_ways([(0, m), (m - 1, n - 1)])
    opposites = [(i, (i + m) % n) for i in range(n) if i not in specials]
    forwards = both_ways([(0, m - 1), (m, n - 1)])

    own = slices[0]
    rows, k = own.shape
    cut = rows // 5 * 4
    cut_special = rows // 5 * 3
    size = rows - cut
    bf16, f32 = jnp.bfloat16, jnp.float32
    pieces = (piece(own, 0, cut_special), piece(own, cut_special, rows - cut_special))
    v = [(VMEM, virt_energy[None, :]), (VMEM, virt_energy[:, None])]
    flops = 12 * rows * rows * k

    prev_near = permute(near_keep.astype(f32), [(i, (i + 1) % n) for i in range(n)])
    straight_slices = [permute(pieces[0], straight), permute(pieces[1], straight)]
    mate = permute(own, mates)
    outer = permute(own, outers)
    small = [(SMEM, x) for x in (order, occ_energy, near_keep, prev_near, far_keep)]

    right = pltpu.VMEM((rows, 3 * k), bf16)
    wide = pltpu.VMEM((rows, 3 * rows), bf16)
    tall = pltpu.VMEM((3 * rows, k), bf16)
    dma = pltpu.SemaphoreType.DMA
    acc, own_three = call(
        kernel_d, [small[0], small[1], (VMEM, own), *v],
        [((rows, k), f32), ((rows, 3 * k), bf16)], [right, wide, tall], flops, 40_000_000,
    )
    (first,), acc = after((straight_slices[1],), acc)
    late1 = permute(first, forwards)
    acc, later = call(
        lambda *refs: kernel_ab("A", *refs),
        [*small, (VMEM, own_three), (VMEM, mate), *v, (VMEM, acc)],
        [((rows, k), f32), ((8, 128), f32)], [right, wide, tall], flops, 40_000_000,
    )
    (whole,), acc = after((own,), acc)
    pieces = (whole[:cut], whole[cut:])
    rest = [permute(piece, opposites) for piece in pieces]
    late = [permute(straight_slices[0], forwards), late1]
    (acc,) = call(
        lambda *refs: kernel_ab("B", *refs),
        [(VMEM, later), (VMEM, own_three), (ANY, outer), *((ANY, x) for x in straight_slices), *v, (VMEM, acc)],
        [((rows, k), f32)], [pltpu.VMEM((rows, k), f32), right, wide, tall, dma], flops, 40_000_000,
    )
    acc, amp_a, tall_a = call(
        kernel_l0,
        [(VMEM, later), (VMEM, own_three), (VMEM, late[0]), (VMEM, late[1]), (VMEM, rest[0]), *v, (VMEM, acc)],
        [((rows, k), f32), ((rows, cut), f32), ((3 * cut, k), bf16)],
        [pltpu.VMEM((cut, 3 * k), bf16), pltpu.VMEM((cut, 3 * cut), bf16)],
        flops // 2,
        26_000_000,
    )
    (acc,) = call(
        kernel_l1,
        [(VMEM, later), (VMEM, own_three), (VMEM, late[1]), (VMEM, rest[1]), *v, (VMEM, acc), (VMEM, amp_a), (VMEM, tall_a)],
        [((rows, k), f32)],
        [
            pltpu.VMEM((size, 3 * k), bf16),
            pltpu.VMEM((3 * size, k), bf16),
            pltpu.VMEM((cut, 3 * size), bf16),
            pltpu.VMEM((size, 3 * cut), bf16),
            pltpu.VMEM((size, 3 * size), bf16),
            pltpu.VMEM((rows, k), f32),
            pltpu.SemaphoreType.DMA((4,)),
        ],
        flops // 2,
        26_000_000,
        [ANY],
    )
    return acc[None]


def solution(mesh):
    return jax.shard_map(
        body,
        mesh=mesh,
        in_specs=(
            P(("frag", "orb"), None, None),
            P("frag"),
            P("frag"),
            P("frag"),
            P(("frag", "orb")),
            P("frag"),
        ),
        out_specs=P(("frag", "orb"), None, None),
        check_vma=False,
    )
```

```python
import jax
import jax.numpy as jnp
from jax import lax
from jax.experimental import pallas as pl
from jax.experimental.pallas import tpu as pltpu
from jax.sharding import PartitionSpec as P


EXTRA = 8
NT = (((1,), (1,)), ((), ()))
NN = (((1,), (0,)), ((), ()))


def permute(block, pairs):
    return lax.ppermute(block, "orb", pairs)


def both_ways(pairs):
    return pairs + [(j, i) for i, j in pairs]


def split(x):
    high = x.astype(jnp.bfloat16)
    low = (x - high.astype(jnp.float32)).astype(jnp.bfloat16)
    return high, low


def put_tall_turned(ref, x):
    high, low = split(x.T)
    k = x.shape[1]
    ref[0:k] = high
    ref[k : 2 * k] = low
    ref[2 * k : 3 * k] = high


def put_across(ref, x):
    high, low = split(x)
    k = x.shape[1]
    ref[:, 0:k] = high
    ref[:, k : 2 * k] = high
    ref[:, 2 * k : 3 * k] = low


def dot(left, right, dims):
    return lax.dot_general(left, right, dims, preferred_element_type=jnp.float32)


def put_tall(ref, x):
    high, low = split(x)
    k = x.shape[0]
    ref[0:k] = high
    ref[k : 2 * k] = high
    ref[2 * k : 3 * k] = low


def put_wide(ref, x):
    high, low = split(x)
    k = x.shape[1]
    ref[:, 0:k] = high
    ref[:, k : 2 * k] = low
    ref[:, 2 * k : 3 * k] = high


def overlap(own, right):
    half = own.shape[0] // 2
    return jnp.concatenate(
        [dot(own[0:half], right[...], NT), dot(own[half:], right[...], NT)], axis=0
    )


def column_blocks(k):
    width = k // 4
    return [slice(i * width, (i + 1) * width) for i in range(4)]


def scalars(slot, order, occ, near, prev_near, far):
    n = lax.axis_size("orb")
    m = n // 2
    pos = lax.axis_index("orb")
    odd = lax.rem(pos, 2) == 1
    half = lax.rem(pos, m)
    special = (half == 0) | (half == m - 1)
    mate = jnp.where(odd, pos - 1, pos + 1)
    outer = lax.rem(jnp.where(odd, pos + 1, pos + n - 1), n)
    opposite = lax.rem(pos + m, n)
    if slot == "D":
        partner, weight = pos, jnp.float32(1.0)
    else:
        near_next = near[0].astype(jnp.float32)
        near_before = prev_near[0]
        mate_weight = jnp.where(odd, near_before, near_next)
        outer_weight = jnp.where(odd, near_next, near_before)
        far_weight = far[half].astype(jnp.float32)
        if slot == "A":
            partner, weight = mate, mate_weight
        else:
            ring = jnp.logical_not(special) if slot == "B" else special
            partner = jnp.where(ring, outer, opposite)
            weight = jnp.where(ring, outer_weight, far_weight)
    return occ[order[pos]] + occ[order[partner]], weight


def case(name):
    n = lax.axis_size("orb")
    m = n // 2
    half = lax.rem(lax.axis_index("orb"), m)
    special = (half == 0) | (half == m - 1)
    return special if name == "special" else jnp.logical_not(special)


def fetch(buffer, sem, sources):
    for name, source in sources:

        @pl.when(case(name))
        def _(source=source):
            copy = pltpu.make_async_copy(source, buffer, sem)
            copy.start()
            copy.wait()


def kernel_d(order, occ, own, vrow, vcol, out, own_three, right, wide, tall):
    k = own.shape[1]
    high, low = split(own[...])
    own_three[:, 0:k] = high
    own_three[:, k : 2 * k] = high
    own_three[:, 2 * k : 3 * k] = low
    put_wide(right, own[...])
    put_tall(tall, own[...])
    total, _ = scalars("D", order, occ, None, None, None)
    put_wide(wide, overlap(own_three, right) / (total - vcol[...] - vrow[...]))
    for columns in column_blocks(k):
        out[:, columns] = dot(wide[...], tall[:, columns], NN)


def kernel_ab(slot, *refs):
    if slot == "A":
        order, occ, near, prev_near, far, own, other, vrow, vcol, acc, out, later, right, wide, tall = refs
        total, weight = scalars("A", order, occ, near, prev_near, far)
        for i, name in enumerate("BL"):
            for j, value in enumerate(scalars(name, order, occ, near, prev_near, far)):
                later[2 * i + j : 2 * i + j + 1] = jnp.full((1, later.shape[1]), value, jnp.float32)
    else:
        later, own, plain, special0, special1, vrow, vcol, acc, out, other, right, wide, tall, sem = refs
        total, weight = later[0:1, 0:1], later[1:2, 0:1]
        cut = special0.shape[0]
        fetch(other, sem, [("plain", plain)])
        fetch(other.at[0:cut], sem, [("special", special0)])
        fetch(other.at[cut:], sem, [("special", special1.at[0 : special1.shape[0] - EXTRA])])
    put_wide(right, other[...])
    put_tall(tall, other[...])
    amp = overlap(own, right) / (total - vcol[...] - vrow[...])
    put_wide(wide, (2.0 * amp - amp.T) * weight)
    for columns in column_blocks(acc.shape[1]):
        out[:, columns] = acc[:, columns] + dot(wide[...], tall[:, columns], NN)


def kernel_t(own, out):
    put_tall_turned(out, own[...])


def late_scalars(later, late1):
    n = lax.axis_size("orb")
    first = lax.rem(lax.axis_index("orb"), n // 2) == 0
    last = late1.shape[0] - EXTRA
    return later[2:3, 0:1], jnp.where(first, late1[last : last + 1, 0:1], later[3:4, 0:1])


def kernel_l0(later, own, late0, late1, rest, vrow, vcol, acc, out, amp_a, tall, right, wide):
    cut = rest.shape[0]
    late = jnp.concatenate([late0[...], late1[0 : cut - late0.shape[0]]], axis=0)
    other = jnp.where(case("special"), late, rest[...])
    put_wide(right, other)
    put_tall(tall, other)
    total, weight = late_scalars(later, late1)
    amp = overlap(own, right) / (total - vcol[...] - vrow[:, 0:cut])
    amp_a[...] = amp
    inner = amp[0:cut]
    put_wide(wide, (2.0 * inner - inner.T) * weight)
    for columns in column_blocks(acc.shape[1]):
        out[0:cut, columns] = acc[0:cut, columns] + dot(wide[...], tall[:, columns], NN)
    out[cut:] = acc[cut:]


def kernel_l1(
    later, own_turned, late, rest, vrow, vcol, acc, amp_a, tall_a,
    out, left, tall, wide_ab, wide_ba, wide_bb, result, out_sems,
):
    cut = amp_a.shape[1]
    size = rest.shape[0]
    last = late.shape[0] - EXTRA
    other = jnp.where(case("special"), late[last - size : last], rest[...])
    put_across(left, other)
    put_tall(tall, other)
    total, weight = late_scalars(later, late)
    turned = dot(left[...], own_turned[...], NN) / (total - vrow[...] - vcol[cut:])
    across = amp_a[cut:]
    put_wide(wide_ab, ((2.0 * turned[:, 0:cut] - across) * weight).T)
    put_wide(wide_ba, (2.0 * across - turned[:, 0:cut]) * weight)
    put_wide(wide_bb, (2.0 * turned[:, cut:].T - turned[:, cut:]) * weight)
    copies = []
    for i, columns in enumerate(column_blocks(acc.shape[1])):
        result[0:cut, columns] = acc[0:cut, columns] + dot(wide_ab[...], tall[:, columns], NN)
        result[cut:, columns] = (
            acc[cut:, columns]
            + dot(wide_ba[...], tall_a[:, columns], NN)
            + dot(wide_bb[...], tall[:, columns], NN)
        )
        copies.append(pltpu.make_async_copy(result.at[:, columns], out.at[:, columns], out_sems.at[i]))
        copies[-1].start()
    for copy in copies:
        copy.wait()


SMEM = pl.BlockSpec(memory_space=pltpu.SMEM)
VMEM = pl.BlockSpec(memory_space=pltpu.VMEM)
ANY = pl.BlockSpec(memory_space=pl.ANY)


def call(kernel, operands, outs, scratch, flops, limit=None, out_specs=None):
    return pl.pallas_call(
        kernel,
        out_shape=[jax.ShapeDtypeStruct(shape, dtype) for shape, dtype in outs],
        in_specs=[spec for spec, _ in operands],
        out_specs=out_specs or [VMEM] * len(outs),
        scratch_shapes=scratch,
        cost_estimate=pl.CostEstimate(flops=flops, bytes_accessed=8_000_000, transcendentals=0),
        compiler_params=pltpu.CompilerParams(vmem_limit_bytes=limit),
    )(*[value for _, value in operands])


def piece(array, start, size, tag=None):
    def kernel(source, *rest):
        *tags, out, sem = rest
        copy = pltpu.make_async_copy(source.at[pl.ds(start, size)], out.at[pl.ds(0, size)], sem)
        copy.start()
        for value in tags:
            out[size:] = jnp.full((EXTRA, out.shape[1]), value[0], out.dtype)
        copy.wait()

    tags = [] if tag is None else [(SMEM, tag)]
    shape = (size + EXTRA * len(tags), array.shape[1])
    return call(kernel, [(ANY, array), *tags], [(shape, array.dtype)], [pltpu.SemaphoreType.DMA], 0, 4_000_000)[0]


def after(values, token):
    *values, token = lax.optimization_barrier((*values, token))
    return values, token


def body(slices, occ_energy, virt_energy, order, near_keep, far_keep):
    n = lax.axis_size("orb")
    m = n // 2
    specials = (0, m - 1, m, n - 1)
    mates = [(i, i ^ 1) for i in range(n)]
    outers = both_ways([(i, i + 1) for i in range(1, n - 1, 2) if i not in specials])
    straight = both_ways([(0, m), (m - 1, n - 1)])
    opposites = [(i, (i + m) % n) for i in range(n) if i not in specials]
    forwards = both_ways([(0, m - 1), (m, n - 1)])

    own = slices[0]
    rows, k = own.shape
    cut = rows // 5 * 4
    cut_special = rows // 5 * 3
    size = rows - cut
    bf16, f32 = jnp.bfloat16, jnp.float32
    near_weight = near_keep.astype(f32)
    pieces = (piece(own, 0, cut_special), piece(own, cut_special, rows - cut_special, near_weight))
    v = [(VMEM, virt_energy[None, :]), (VMEM, virt_energy[:, None])]
    flops = 12 * rows * rows * k

    prev_near = permute(near_weight, [(i, i + 1) for i in range(n) if i not in (m - 1, n - 1)])
    straight_slices = [permute(pieces[0], straight), permute(pieces[1], straight)]
    mate = permute(own, mates)
    outer = permute(own, outers)
    small = [(SMEM, x) for x in (order, occ_energy, near_keep, prev_near, far_keep)]

    right = pltpu.VMEM((rows, 3 * k), bf16)
    wide = pltpu.VMEM((rows, 3 * rows), bf16)
    tall = pltpu.VMEM((3 * rows, k), bf16)
    dma = pltpu.SemaphoreType.DMA
    acc, own_three = call(
        kernel_d, [small[0], small[1], (VMEM, own), *v],
        [((rows, k), f32), ((rows, 3 * k), bf16)], [right, wide, tall], flops, 32_000_000,
    )
    (first,), acc = after((straight_slices[1],), acc)
    late1 = permute(first, forwards)
    acc, later = call(
        lambda *refs: kernel_ab("A", *refs),
        [*small, (VMEM, own_three), (VMEM, mate), *v, (VMEM, acc)],
        [((rows, k), f32), ((8, 128), f32)], [right, wide, tall], flops, 32_000_000,
    )
    (whole,), acc = after((own,), acc)
    pieces = (whole[:cut], whole[cut:])
    rest = [permute(piece, opposites) for piece in pieces]
    late = [permute(straight_slices[0], forwards), late1]
    (acc,) = call(
        lambda *refs: kernel_ab("B", *refs),
        [(VMEM, later), (VMEM, own_three), (ANY, outer), *((ANY, x) for x in straight_slices), *v, (VMEM, acc)],
        [((rows, k), f32)], [pltpu.VMEM((rows, k), f32), right, wide, tall, dma], flops, 32_000_000,
    )
    (whole,), acc = after((own,), acc)
    (own_turned,) = call(kernel_t, [(VMEM, whole)], [((3 * k, rows), bf16)], [], 0, 20_000_000)
    acc, amp_a, tall_a = call(
        kernel_l0,
        [(VMEM, later), (VMEM, own_three), (VMEM, late[0]), (VMEM, late[1]), (VMEM, rest[0]), *v, (VMEM, acc)],
        [((rows, k), f32), ((rows, cut), f32), ((3 * cut, k), bf16)],
        [pltpu.VMEM((cut, 3 * k), bf16), pltpu.VMEM((cut, 3 * cut), bf16)],
        flops // 2,
        26_000_000,
    )
    (acc,) = call(
        kernel_l1,
        [(VMEM, later), (VMEM, own_turned), (VMEM, late[1]), (VMEM, rest[1]), *v, (VMEM, acc), (VMEM, amp_a), (VMEM, tall_a)],
        [((rows, k), f32)],
        [
            pltpu.VMEM((size, 3 * k), bf16),
            pltpu.VMEM((3 * size, k), bf16),
            pltpu.VMEM((cut, 3 * size), bf16),
            pltpu.VMEM((size, 3 * cut), bf16),
            pltpu.VMEM((size, 3 * size), bf16),
            pltpu.VMEM((rows, k), f32),
            pltpu.SemaphoreType.DMA((4,)),
        ],
        flops // 2,
        26_000_000,
        [ANY],
    )
    return acc[None]


def solution(mesh):
    return jax.shard_map(
        body,
        mesh=mesh,
        in_specs=(
            P(("frag", "orb"), None, None),
            P("frag"),
            P("frag"),
            P("frag"),
            P(("frag", "orb")),
            P("frag"),
        ),
        out_specs=P(("frag", "orb"), None, None),
        check_vma=False,
    )
```

```python
import jax
import jax.numpy as jnp
from jax import lax
from jax.experimental import pallas as pl
from jax.experimental.pallas import tpu as pltpu
from jax.sharding import PartitionSpec as P


EXTRA = 8
NT = (((1,), (1,)), ((), ()))
NN = (((1,), (0,)), ((), ()))


def permute(block, pairs):
    return lax.ppermute(block, "orb", pairs)


def both_ways(pairs):
    return pairs + [(j, i) for i, j in pairs]


def split(x):
    high = x.astype(jnp.bfloat16)
    low = (x - high.astype(jnp.float32)).astype(jnp.bfloat16)
    return high, low


def put_tall_turned(ref, x):
    high, low = split(x.T)
    k = x.shape[1]
    ref[0:k] = high
    ref[k : 2 * k] = low
    ref[2 * k : 3 * k] = high


def put_across(ref, x):
    high, low = split(x)
    k = x.shape[1]
    ref[:, 0:k] = high
    ref[:, k : 2 * k] = high
    ref[:, 2 * k : 3 * k] = low


def dot(left, right, dims):
    return lax.dot_general(left, right, dims, preferred_element_type=jnp.float32)


def put_tall(ref, x):
    high, low = split(x)
    k = x.shape[0]
    ref[0:k] = high
    ref[k : 2 * k] = high
    ref[2 * k : 3 * k] = low


def put_wide(ref, x):
    high, low = split(x)
    k = x.shape[1]
    ref[:, 0:k] = high
    ref[:, k : 2 * k] = low
    ref[:, 2 * k : 3 * k] = high


def overlap(own, right):
    half = own.shape[0] // 2
    return jnp.concatenate(
        [dot(own[0:half], right[...], NT), dot(own[half:], right[...], NT)], axis=0
    )


def column_blocks(k):
    width = k // 4
    return [slice(i * width, (i + 1) * width) for i in range(4)]


def scalars(slot, order, occ, near, prev_near, far):
    n = lax.axis_size("orb")
    m = n // 2
    pos = lax.axis_index("orb")
    odd = lax.rem(pos, 2) == 1
    half = lax.rem(pos, m)
    special = (half == 0) | (half == m - 1)
    mate = jnp.where(odd, pos - 1, pos + 1)
    outer = lax.rem(jnp.where(odd, pos + 1, pos + n - 1), n)
    opposite = lax.rem(pos + m, n)
    if slot == "D":
        partner, weight = pos, jnp.float32(1.0)
    else:
        near_next = near[0].astype(jnp.float32)
        near_before = prev_near[0]
        mate_weight = jnp.where(odd, near_before, near_next)
        outer_weight = jnp.where(odd, near_next, near_before)
        far_weight = far[half].astype(jnp.float32)
        if slot == "A":
            partner, weight = mate, mate_weight
        else:
            ring = jnp.logical_not(special) if slot == "B" else special
            partner = jnp.where(ring, outer, opposite)
            weight = jnp.where(ring, outer_weight, far_weight)
    return occ[order[pos]] + occ[order[partner]], weight


def case(name):
    n = lax.axis_size("orb")
    m = n // 2
    half = lax.rem(lax.axis_index("orb"), m)
    special = (half == 0) | (half == m - 1)
    return special if name == "special" else jnp.logical_not(special)


def fetch(buffer, sem, sources):
    for name, source in sources:

        @pl.when(case(name))
        def _(source=source):
            copy = pltpu.make_async_copy(source, buffer, sem)
            copy.start()
            copy.wait()


def kernel_d(order, occ, own, vrow, vcol, out, own_three, right, wide, tall):
    k = own.shape[1]
    high, low = split(own[...])
    own_three[:, 0:k] = high
    own_three[:, k : 2 * k] = high
    own_three[:, 2 * k : 3 * k] = low
    put_wide(right, own[...])
    put_tall(tall, own[...])
    total, _ = scalars("D", order, occ, None, None, None)
    put_wide(wide, overlap(own_three, right) / (total - vcol[...] - vrow[...]))
    for columns in column_blocks(k):
        out[:, columns] = dot(wide[...], tall[:, columns], NN)


def kernel_ab(slot, *refs):
    if slot == "A":
        order, occ, near, prev_near, far, own, other, vrow, vcol, acc, out, later, right, wide, tall = refs
        total, weight = scalars("A", order, occ, near, prev_near, far)
        for i, name in enumerate("BL"):
            for j, value in enumerate(scalars(name, order, occ, near, prev_near, far)):
                later[2 * i + j : 2 * i + j + 1] = jnp.full((1, later.shape[1]), value, jnp.float32)
    else:
        later, own, plain, special0, special1, vrow, vcol, acc, out, other, right, wide, tall, sem = refs
        total, weight = later[0:1, 0:1], later[1:2, 0:1]
        cut = special0.shape[0]
        fetch(other, sem, [("plain", plain)])
        fetch(other.at[0:cut], sem, [("special", special0)])
        fetch(other.at[cut:], sem, [("special", special1.at[0 : special1.shape[0] - EXTRA])])
    put_wide(right, other[...])
    put_tall(tall, other[...])
    amp = overlap(own, right) / (total - vcol[...] - vrow[...])
    put_wide(wide, (2.0 * amp - amp.T) * weight)
    for columns in column_blocks(acc.shape[1]):
        out[:, columns] = acc[:, columns] + dot(wide[...], tall[:, columns], NN)


def kernel_t(own, out):
    put_tall_turned(out, own[...])


def late_scalars(later, late1):
    n = lax.axis_size("orb")
    first = lax.rem(lax.axis_index("orb"), n // 2) == 0
    last = late1.shape[0] - EXTRA
    return later[2:3, 0:1], jnp.where(first, late1[last : last + 1, 0:1], later[3:4, 0:1])


def kernel_l0(later, own, late0, late1, rest, vrow, vcol, acc, out, amp_a, tall, right, wide):
    cut = rest.shape[0]
    late = jnp.concatenate([late0[...], late1[0 : cut - late0.shape[0]]], axis=0)
    other = jnp.where(case("special"), late, rest[...])
    put_wide(right, other)
    put_tall(tall, other)
    total, weight = late_scalars(later, late1)
    amp = overlap(own, right) / (total - vcol[...] - vrow[:, 0:cut])
    amp_a[...] = amp
    inner = amp[0:cut]
    put_wide(wide, (2.0 * inner - inner.T) * weight)
    for columns in column_blocks(acc.shape[1]):
        out[0:cut, columns] = acc[0:cut, columns] + dot(wide[...], tall[:, columns], NN)
    out[cut:] = acc[cut:]


def kernel_l1(
    later, own_turned, late, rest, vrow, vcol, acc, amp_a, tall_a,
    out, left, tall, wide_ab, wide_ba, wide_bb, result, out_sems,
):
    cut = amp_a.shape[1]
    size = rest.shape[0]
    last = late.shape[0] - EXTRA
    other = jnp.where(case("special"), late[last - size : last], rest[...])
    put_across(left, other)
    put_tall(tall, other)
    total, weight = late_scalars(later, late)
    turned = dot(left[...], own_turned[...], NN) / (total - vrow[...] - vcol[cut:])
    across = amp_a[cut:]
    put_wide(wide_ab, ((2.0 * turned[:, 0:cut] - across) * weight).T)
    put_wide(wide_ba, (2.0 * across - turned[:, 0:cut]) * weight)
    put_wide(wide_bb, (2.0 * turned[:, cut:].T - turned[:, cut:]) * weight)
    copies = []
    for i, columns in enumerate(column_blocks(acc.shape[1])):
        result[0:cut, columns] = acc[0:cut, columns] + dot(wide_ab[...], tall[:, columns], NN)
        copies.append(
            pltpu.make_async_copy(
                result.at[0:cut, columns], out.at[0:cut, columns], out_sems.at[2 * i]
            )
        )
        copies[-1].start()
        result[cut:, columns] = (
            acc[cut:, columns]
            + dot(wide_ba[...], tall_a[:, columns], NN)
            + dot(wide_bb[...], tall[:, columns], NN)
        )
        copies.append(
            pltpu.make_async_copy(
                result.at[cut:, columns], out.at[cut:, columns], out_sems.at[2 * i + 1]
            )
        )
        copies[-1].start()
    for copy in copies:
        copy.wait()


SMEM = pl.BlockSpec(memory_space=pltpu.SMEM)
VMEM = pl.BlockSpec(memory_space=pltpu.VMEM)
ANY = pl.BlockSpec(memory_space=pl.ANY)


def call(kernel, operands, outs, scratch, flops, limit=None, out_specs=None):
    return pl.pallas_call(
        kernel,
        out_shape=[jax.ShapeDtypeStruct(shape, dtype) for shape, dtype in outs],
        in_specs=[spec for spec, _ in operands],
        out_specs=out_specs or [VMEM] * len(outs),
        scratch_shapes=scratch,
        cost_estimate=pl.CostEstimate(flops=flops, bytes_accessed=8_000_000, transcendentals=0),
        compiler_params=pltpu.CompilerParams(vmem_limit_bytes=limit),
    )(*[value for _, value in operands])


def piece(array, start, size, tag=None):
    def kernel(source, *rest):
        *tags, out, sem = rest
        copy = pltpu.make_async_copy(source.at[pl.ds(start, size)], out.at[pl.ds(0, size)], sem)
        copy.start()
        for value in tags:
            out[size:] = jnp.full((EXTRA, out.shape[1]), value[0], out.dtype)
        copy.wait()

    tags = [] if tag is None else [(SMEM, tag)]
    shape = (size + EXTRA * len(tags), array.shape[1])
    return call(kernel, [(ANY, array), *tags], [(shape, array.dtype)], [pltpu.SemaphoreType.DMA], 0, 4_000_000)[0]


def after(values, token):
    *values, token = lax.optimization_barrier((*values, token))
    return values, token


def body(slices, occ_energy, virt_energy, order, near_keep, far_keep):
    n = lax.axis_size("orb")
    m = n // 2
    specials = (0, m - 1, m, n - 1)
    mates = [(i, i ^ 1) for i in range(n)]
    outers = both_ways([(i, i + 1) for i in range(1, n - 1, 2) if i not in specials])
    straight = both_ways([(0, m), (m - 1, n - 1)])
    opposites = [(i, (i + m) % n) for i in range(n) if i not in specials]
    forwards = both_ways([(0, m - 1), (m, n - 1)])

    own = slices[0]
    rows, k = own.shape
    cut = rows // 5 * 4
    cut_special = rows // 5 * 3
    size = rows - cut
    bf16, f32 = jnp.bfloat16, jnp.float32
    near_weight = near_keep.astype(f32)
    pieces = (piece(own, 0, cut_special), piece(own, cut_special, rows - cut_special, near_weight))
    v = [(VMEM, virt_energy[None, :]), (VMEM, virt_energy[:, None])]
    flops = 12 * rows * rows * k

    prev_near = permute(near_weight, [(i, i + 1) for i in range(n) if i not in (m - 1, n - 1)])
    straight_slices = [permute(pieces[0], straight), permute(pieces[1], straight)]
    mate = permute(own, mates)
    outer = permute(own, outers)
    small = [(SMEM, x) for x in (order, occ_energy, near_keep, prev_near, far_keep)]

    right = pltpu.VMEM((rows, 3 * k), bf16)
    wide = pltpu.VMEM((rows, 3 * rows), bf16)
    tall = pltpu.VMEM((3 * rows, k), bf16)
    dma = pltpu.SemaphoreType.DMA
    acc, own_three = call(
        kernel_d, [small[0], small[1], (VMEM, own), *v],
        [((rows, k), f32), ((rows, 3 * k), bf16)], [right, wide, tall], flops, 32_000_000,
    )
    (first,), acc = after((straight_slices[1],), acc)
    late1 = permute(first, forwards)
    acc, later = call(
        lambda *refs: kernel_ab("A", *refs),
        [*small, (VMEM, own_three), (VMEM, mate), *v, (VMEM, acc)],
        [((rows, k), f32), ((8, 128), f32)], [right, wide, tall], flops, 32_000_000,
    )
    (whole,), acc = after((own,), acc)
    pieces = (whole[:cut], whole[cut:])
    rest = [permute(piece, opposites) for piece in pieces]
    late = [permute(straight_slices[0], forwards), late1]
    (acc,) = call(
        lambda *refs: kernel_ab("B", *refs),
        [(VMEM, later), (VMEM, own_three), (ANY, outer), *((ANY, x) for x in straight_slices), *v, (VMEM, acc)],
        [((rows, k), f32)], [pltpu.VMEM((rows, k), f32), right, wide, tall, dma], flops, 32_000_000,
    )
    (whole,), acc = after((own,), acc)
    (own_turned,) = call(kernel_t, [(VMEM, whole)], [((3 * k, rows), bf16)], [], 0, 20_000_000)
    acc, amp_a, tall_a = call(
        kernel_l0,
        [(VMEM, later), (VMEM, own_three), (VMEM, late[0]), (VMEM, late[1]), (VMEM, rest[0]), *v, (VMEM, acc)],
        [((rows, k), f32), ((rows, cut), f32), ((3 * cut, k), bf16)],
        [pltpu.VMEM((cut, 3 * k), bf16), pltpu.VMEM((cut, 3 * cut), bf16)],
        flops // 2,
        26_000_000,
    )
    (acc,) = call(
        kernel_l1,
        [(VMEM, later), (VMEM, own_turned), (VMEM, late[1]), (VMEM, rest[1]), *v, (VMEM, acc), (VMEM, amp_a), (VMEM, tall_a)],
        [((rows, k), f32)],
        [
            pltpu.VMEM((size, 3 * k), bf16),
            pltpu.VMEM((3 * size, k), bf16),
            pltpu.VMEM((cut, 3 * size), bf16),
            pltpu.VMEM((size, 3 * cut), bf16),
            pltpu.VMEM((size, 3 * size), bf16),
            pltpu.VMEM((rows, k), f32),
            pltpu.SemaphoreType.DMA((8,)),
        ],
        flops // 2,
        26_000_000,
        [ANY],
    )
    return acc[None]


def solution(mesh):
    return jax.shard_map(
        body,
        mesh=mesh,
        in_specs=(
            P(("frag", "orb"), None, None),
            P("frag"),
            P("frag"),
            P("frag"),
            P(("frag", "orb")),
            P("frag"),
        ),
        out_specs=P(("frag", "orb"), None, None),
        check_vma=False,
    )
```

```python
import jax
import jax.numpy as jnp
from jax import lax
from jax.experimental import pallas as pl
from jax.experimental.pallas import tpu as pltpu
from jax.sharding import PartitionSpec as P


EXTRA = 8
NT = (((1,), (1,)), ((), ()))
NN = (((1,), (0,)), ((), ()))


def permute(block, pairs):
    return lax.ppermute(block, "orb", pairs)


def both_ways(pairs):
    return pairs + [(j, i) for i, j in pairs]


def split(x):
    high = x.astype(jnp.bfloat16)
    low = (x - high.astype(jnp.float32)).astype(jnp.bfloat16)
    return high, low


def put_tall_turned(ref, x):
    high, low = split(x.T)
    k = x.shape[1]
    ref[0:k] = high
    ref[k : 2 * k] = low
    ref[2 * k : 3 * k] = high


def put_across(ref, x):
    high, low = split(x)
    k = x.shape[1]
    ref[:, 0:k] = high
    ref[:, k : 2 * k] = high
    ref[:, 2 * k : 3 * k] = low


def dot(left, right, dims):
    return lax.dot_general(left, right, dims, preferred_element_type=jnp.float32)


def put_tall(ref, x):
    high, low = split(x)
    k = x.shape[0]
    ref[0:k] = high
    ref[k : 2 * k] = high
    ref[2 * k : 3 * k] = low


def put_wide(ref, x):
    high, low = split(x)
    k = x.shape[1]
    ref[:, 0:k] = high
    ref[:, k : 2 * k] = low
    ref[:, 2 * k : 3 * k] = high


def overlap(own, right):
    half = own.shape[0] // 2
    return jnp.concatenate(
        [dot(own[0:half], right[...], NT), dot(own[half:], right[...], NT)], axis=0
    )


def column_blocks(k):
    width = k // 4
    return [slice(i * width, (i + 1) * width) for i in range(4)]


def scalars(slot, order, occ, near, prev_near, far):
    n = lax.axis_size("orb")
    m = n // 2
    pos = lax.axis_index("orb")
    odd = lax.rem(pos, 2) == 1
    half = lax.rem(pos, m)
    special = (half == 0) | (half == m - 1)
    mate = jnp.where(odd, pos - 1, pos + 1)
    outer = lax.rem(jnp.where(odd, pos + 1, pos + n - 1), n)
    opposite = lax.rem(pos + m, n)
    if slot == "D":
        partner, weight = pos, jnp.float32(1.0)
    else:
        near_next = near[0].astype(jnp.float32)
        near_before = prev_near[0]
        mate_weight = jnp.where(odd, near_before, near_next)
        outer_weight = jnp.where(odd, near_next, near_before)
        far_weight = far[half].astype(jnp.float32)
        if slot == "A":
            partner, weight = mate, mate_weight
        else:
            ring = jnp.logical_not(special) if slot == "B" else special
            partner = jnp.where(ring, outer, opposite)
            weight = jnp.where(ring, outer_weight, far_weight)
    return occ[order[pos]] + occ[order[partner]], weight


def case(name):
    n = lax.axis_size("orb")
    m = n // 2
    half = lax.rem(lax.axis_index("orb"), m)
    special = (half == 0) | (half == m - 1)
    return special if name == "special" else jnp.logical_not(special)


def fetch(buffer, sem, sources):
    for name, source in sources:

        @pl.when(case(name))
        def _(source=source):
            copy = pltpu.make_async_copy(source, buffer, sem)
            copy.start()
            copy.wait()


def kernel_d(order, occ, own, vrow, vcol, out, own_three, right, wide, tall):
    k = own.shape[1]
    high, low = split(own[...])
    own_three[:, 0:k] = high
    own_three[:, k : 2 * k] = high
    own_three[:, 2 * k : 3 * k] = low
    put_wide(right, own[...])
    put_tall(tall, own[...])
    total, _ = scalars("D", order, occ, None, None, None)
    put_wide(wide, overlap(own_three, right) / (total - vcol[...] - vrow[...]))
    for columns in column_blocks(k):
        out[:, columns] = dot(wide[...], tall[:, columns], NN)


def kernel_ab(slot, *refs):
    if slot == "A":
        order, occ, near, prev_near, far, own, other, vrow, vcol, acc, out, later, right, wide, tall = refs
        total, weight = scalars("A", order, occ, near, prev_near, far)
        for i, name in enumerate("BL"):
            for j, value in enumerate(scalars(name, order, occ, near, prev_near, far)):
                later[2 * i + j : 2 * i + j + 1] = jnp.full((1, later.shape[1]), value, jnp.float32)
    else:
        later, own, plain, special0, special1, vrow, vcol, acc, out, other, right, wide, tall, sem = refs
        total, weight = later[0:1, 0:1], later[1:2, 0:1]
        cut = special0.shape[0]
        fetch(other, sem, [("plain", plain)])
        fetch(other.at[0:cut], sem, [("special", special0)])
        fetch(other.at[cut:], sem, [("special", special1.at[0 : special1.shape[0] - EXTRA])])
    put_wide(right, other[...])
    put_tall(tall, other[...])
    amp = overlap(own, right) / (total - vcol[...] - vrow[...])
    put_wide(wide, (2.0 * amp - amp.T) * weight)
    for columns in column_blocks(acc.shape[1]):
        out[:, columns] = acc[:, columns] + dot(wide[...], tall[:, columns], NN)


def kernel_t(own, out):
    put_tall_turned(out, own[...])


def late_scalars(later, late1):
    n = lax.axis_size("orb")
    first = lax.rem(lax.axis_index("orb"), n // 2) == 0
    last = late1.shape[0] - EXTRA
    return later[2:3, 0:1], jnp.where(first, late1[last : last + 1, 0:1], later[3:4, 0:1])


def kernel_l0(later, own, late0, late1, rest, vrow, vcol, acc, out, amp_a, tall, right, wide):
    cut = rest.shape[0]
    late = jnp.concatenate([late0[...], late1[0 : cut - late0.shape[0]]], axis=0)
    other = jnp.where(case("special"), late, rest[...])
    put_wide(right, other)
    put_tall(tall, other)
    total, weight = late_scalars(later, late1)
    amp = overlap(own, right) / (total - vcol[...] - vrow[:, 0:cut])
    amp_a[...] = amp
    inner = amp[0:cut]
    put_wide(wide, (2.0 * inner - inner.T) * weight)
    for columns in column_blocks(acc.shape[1]):
        out[0:cut, columns] = acc[0:cut, columns] + dot(wide[...], tall[:, columns], NN)
    out[cut:] = acc[cut:]


def kernel_l1(
    later, own_turned, late, rest, vrow, vcol, acc, amp_a, tall_a,
    out, left, tall, wide_ab, wide_ba, wide_bb, result, out_sems,
):
    cut = amp_a.shape[1]
    size = rest.shape[0]
    last = late.shape[0] - EXTRA
    other = jnp.where(case("special"), late[last - size : last], rest[...])
    put_across(left, other)
    put_tall(tall, other)
    total, weight = late_scalars(later, late)
    turned = dot(left[...], own_turned[...], NN) / (total - vrow[...] - vcol[cut:])
    across = amp_a[cut:]
    put_wide(wide_ab, ((2.0 * turned[:, 0:cut] - across) * weight).T)
    put_wide(wide_ba, (2.0 * across - turned[:, 0:cut]) * weight)
    put_wide(wide_bb, (2.0 * turned[:, cut:].T - turned[:, cut:]) * weight)
    copies = []
    for i, columns in enumerate(column_blocks(acc.shape[1])):
        result[0:cut, columns] = acc[0:cut, columns] + dot(wide_ab[...], tall[:, columns], NN)
        result[cut:, columns] = (
            acc[cut:, columns]
            + dot(wide_ba[...], tall_a[:, columns], NN)
            + dot(wide_bb[...], tall[:, columns], NN)
        )
        copies.append(pltpu.make_async_copy(result.at[:, columns], out.at[:, columns], out_sems.at[i]))
        copies[-1].start()
    for copy in copies:
        copy.wait()


SMEM = pl.BlockSpec(memory_space=pltpu.SMEM)
VMEM = pl.BlockSpec(memory_space=pltpu.VMEM)
ANY = pl.BlockSpec(memory_space=pl.ANY)


def call(kernel, operands, outs, scratch, flops, limit=None, out_specs=None):
    return pl.pallas_call(
        kernel,
        out_shape=[jax.ShapeDtypeStruct(shape, dtype) for shape, dtype in outs],
        in_specs=[spec for spec, _ in operands],
        out_specs=out_specs or [VMEM] * len(outs),
        scratch_shapes=scratch,
        cost_estimate=pl.CostEstimate(flops=flops, bytes_accessed=8_000_000, transcendentals=0),
        compiler_params=pltpu.CompilerParams(vmem_limit_bytes=limit),
    )(*[value for _, value in operands])


def piece(array, start, size, tag=None):
    def kernel(source, *rest):
        *tags, out, sem = rest
        copy = pltpu.make_async_copy(source.at[pl.ds(start, size)], out.at[pl.ds(0, size)], sem)
        copy.start()
        for value in tags:
            out[size:] = jnp.full((EXTRA, out.shape[1]), value[0], out.dtype)
        copy.wait()

    tags = [] if tag is None else [(SMEM, tag)]
    shape = (size + EXTRA * len(tags), array.shape[1])
    return call(kernel, [(ANY, array), *tags], [(shape, array.dtype)], [pltpu.SemaphoreType.DMA], 0, 4_000_000)[0]


def after(values, token):
    *values, token = lax.optimization_barrier((*values, token))
    return values, token


def body(slices, occ_energy, virt_energy, order, near_keep, far_keep):
    n = lax.axis_size("orb")
    m = n // 2
    specials = (0, m - 1, m, n - 1)
    mates = [(i, i ^ 1) for i in range(n)]
    outers = both_ways([(i, i + 1) for i in range(1, n - 1, 2) if i not in specials])
    straight = both_ways([(0, m), (m - 1, n - 1)])
    opposites = [(i, (i + m) % n) for i in range(n) if i not in specials]
    forwards = both_ways([(0, m - 1), (m, n - 1)])

    own = slices[0]
    rows, k = own.shape
    cut = rows // 5 * 4
    cut_special = rows // 5 * 3
    size = rows - cut
    bf16, f32 = jnp.bfloat16, jnp.float32
    near_weight = near_keep.astype(f32)
    pieces = (piece(own, 0, cut_special), piece(own, cut_special, rows - cut_special, near_weight))
    v = [(VMEM, virt_energy[None, :]), (VMEM, virt_energy[:, None])]
    flops = 12 * rows * rows * k

    prev_near = permute(near_weight, [(i, i + 1) for i in range(n) if i not in (m - 1, n - 1)])
    straight_slices = [permute(pieces[0], straight), permute(pieces[1], straight)]
    mate = permute(own, mates)
    outer = permute(own, outers)
    small = [(SMEM, x) for x in (order, occ_energy, near_keep, prev_near, far_keep)]

    right = pltpu.VMEM((rows, 3 * k), bf16)
    wide = pltpu.VMEM((rows, 3 * rows), bf16)
    tall = pltpu.VMEM((3 * rows, k), bf16)
    dma = pltpu.SemaphoreType.DMA
    acc, own_three = call(
        kernel_d, [small[0], small[1], (VMEM, own), *v],
        [((rows, k), f32), ((rows, 3 * k), bf16)], [right, wide, tall], flops, 32_000_000,
    )
    (first, whole), acc = after((straight_slices[1], own), acc)
    pieces, acc = after((whole[:cut], whole[cut:]), acc)
    late1 = permute(first, forwards)
    acc, later = call(
        lambda *refs: kernel_ab("A", *refs),
        [*small, (VMEM, own_three), (VMEM, mate), *v, (VMEM, acc)],
        [((rows, k), f32), ((8, 128), f32)], [right, wide, tall], flops, 32_000_000,
    )
    pieces, acc = after(pieces, acc)
    rest = [permute(piece, opposites) for piece in pieces]
    late = [permute(straight_slices[0], forwards), late1]
    (acc,) = call(
        lambda *refs: kernel_ab("B", *refs),
        [(VMEM, later), (VMEM, own_three), (ANY, outer), *((ANY, x) for x in straight_slices), *v, (VMEM, acc)],
        [((rows, k), f32)], [pltpu.VMEM((rows, k), f32), right, wide, tall, dma], flops, 32_000_000,
    )
    (whole,), acc = after((own,), acc)
    (own_turned,) = call(kernel_t, [(VMEM, whole)], [((3 * k, rows), bf16)], [], 0, 20_000_000)
    acc, amp_a, tall_a = call(
        kernel_l0,
        [(VMEM, later), (VMEM, own_three), (VMEM, late[0]), (VMEM, late[1]), (VMEM, rest[0]), *v, (VMEM, acc)],
        [((rows, k), f32), ((rows, cut), f32), ((3 * cut, k), bf16)],
        [pltpu.VMEM((cut, 3 * k), bf16), pltpu.VMEM((cut, 3 * cut), bf16)],
        flops // 2,
        26_000_000,
    )
    (acc,) = call(
        kernel_l1,
        [(VMEM, later), (VMEM, own_turned), (VMEM, late[1]), (VMEM, rest[1]), *v, (VMEM, acc), (VMEM, amp_a), (VMEM, tall_a)],
        [((rows, k), f32)],
        [
            pltpu.VMEM((size, 3 * k), bf16),
            pltpu.VMEM((3 * size, k), bf16),
            pltpu.VMEM((cut, 3 * size), bf16),
            pltpu.VMEM((size, 3 * cut), bf16),
            pltpu.VMEM((size, 3 * size), bf16),
            pltpu.VMEM((rows, k), f32),
            pltpu.SemaphoreType.DMA((4,)),
        ],
        flops // 2,
        26_000_000,
        [ANY],
    )
    return acc[None]


def solution(mesh):
    return jax.shard_map(
        body,
        mesh=mesh,
        in_specs=(
            P(("frag", "orb"), None, None),
            P("frag"),
            P("frag"),
            P("frag"),
            P(("frag", "orb")),
            P("frag"),
        ),
        out_specs=P(("frag", "orb"), None, None),
        check_vma=False,
    )
```
